256 devices in a mesh: req: 4 (over y), vocab: 64 (over z, x, core).
Axes of the slice: x: 4, y: 4, z: 8, core: 2. Of those that a mesh axis runs over, the one named last changes fastest.
Arguments:
- hidden: bfloat16 [8192, 4096], P('req', 'vocab'), may hold values from -320 to 320
- gain: float32 [4096], replicated, may hold values from 0.5 to 1.5
- head: bfloat16 [4096, 32768], P(None, ('req', 'vocab'))
- targets: int32 [8192], P('req'), may hold values from 0 to 32767
- lengths: int32 [4, 4], P('req'), may hold values from 1 to 1280, 2048 in all within a row
Outputs:
- token_logprob: float32 [8192], P(('req', 'vocab'))
- token_entropy: float32 [8192], P(('req', 'vocab'))
- seq_logprob: float32 [12], P('req')
- seq_entropy: float32 [12], P('req')
The draws below stay inside these ranges and needn't reach their ends.
Inputs may be any that keep to these rules, and one draw needn't show every extreme that they name: lengths[q, 3] counts the empty slots at the end of index q's rows.
All inputs are finite; a program needn't handle non-finite values.
Results may differ from the reference program's by a relative error of at most 0.0012.
Values may be sent and summed in bfloat16 or wider, within the bound.
A program may use at most 128 MiB of HBM per device.

```python
import math
import jax
import jax.numpy as jnp
import numpy as np
from jax import lax

D = 4096
VOCAB = 32768
SEQ_DEV = 3
ROWS_DEV = 2048
ROWS = 8192
SEQS = 12
MOST = 1280
N_REQ = 4


def base_hidden(key):
    noise = jax.random.normal(jax.random.fold_in(key, 1), (ROWS, D), jnp.float32)
    row_scale = jnp.exp(jax.random.uniform(jax.random.fold_in(key, 2), (ROWS,), jnp.float32, 0.0, math.log(10.0)))
    col_rough = jax.random.uniform(jax.random.fold_in(key, 3), (D,), jnp.float32, 0.6, 1.4)
    col_scale = jnp.exp(jnp.arange(D, dtype=jnp.float32) * (math.log(3.0) / D)) * col_rough
    return noise * row_scale[:, None] * col_scale[None, :]


def draw_hidden(key, part):
    return base_hidden(jax.random.fold_in(key, 11)).astype(jnp.bfloat16)


def draw_head(key, part):
    weights = jax.random.normal(jax.random.fold_in(key, 23), (D, VOCAB), jnp.float32) * (3.0 / math.sqrt(D))
    return weights.astype(jnp.bfloat16)


def touch_ends(values, stream_key, smallest, top_value):
    dims = values.shape
    spot = [jax.random.randint(jax.random.fold_in(stream_key, axis), (), 0, dims[axis]) for axis in range(len(dims))]
    values = values.at[tuple(spot)].set(smallest)
    longest = dims.index(max(dims))
    spot[longest] = (spot[longest] + 1) % dims[longest]
    return values.at[tuple(spot)].set(top_value)


def rank_bounds(number_of, lean):
    loads = [(1 << 20) // math.isqrt(grade ** lean) + 1 for grade in range(1, number_of + 1)]
    scale = 1 + sum(loads) // (1 << 30)
    return np.cumsum(np.array([max(1, weight // scale) for weight in loads]))


def ranked_ids(own_key, dims, amount, skew):
    table = rank_bounds(amount, skew)
    ticket = jax.random.randint(jax.random.fold_in(own_key, 1), dims, 0, int(table[amount - 1]))
    rank = jnp.searchsorted(jnp.asarray(table, jnp.int32), ticket, side="right")
    return jax.random.permutation(jax.random.fold_in(own_key, 2), amount)[rank].astype(jnp.int32)


def split_up(number_of, total, limit, lean):
    loads = [(1 << 20) // math.isqrt(grade ** lean) + 1 for grade in range(2, number_of + 1)]
    surplus, given = total - limit - (number_of - 1), [1] * (number_of - 1)
    while surplus > 0:
        free = [i for i in range(number_of - 1) if given[i] < limit]
        mass, remaining = sum([loads[i] for i in free]), surplus
        for i in free:
            extra = min(limit - given[i], max(1, remaining * loads[i] // mass), surplus)
            given[i] = given[i] + extra
            surplus = surplus - extra
    return np.array([limit] + given)


def uneven(stream_key, amount, total, bound, slope):
    if amount == 2:
        one = jax.random.randint(stream_key, (), max(1, total - bound), min(bound, total - 1) + 1)
        return jnp.stack([one, total - one])
    sizes = jnp.asarray(split_up(amount, total, bound, slope), jnp.int32)
    couples = (amount - 1) // 2
    donor, receiver = sizes[1:1 + 2 * couples:2], sizes[2:2 + 2 * couples:2]
    slack = jnp.minimum(donor - 1, bound - receiver)
    shifted = jax.random.randint(jax.random.fold_in(stream_key, 1), (couples,), 0, 1 << 20) % (slack + 1)
    sizes = sizes.at[1:1 + 2 * couples:2].set(donor - shifted).at[2:2 + 2 * couples:2].set(receiver + shifted)
    return sizes[jax.random.permutation(jax.random.fold_in(stream_key, 2), amount)]


def setup_inputs(seed: int = 0) -> dict:
    arg_keys = jax.random.split(jax.random.key(seed), 6)
    hidden = draw_hidden(jax.random.fold_in(arg_keys[5], 71), 0)
    gain = jnp.clip(1.0 + 0.1 * jax.random.normal(arg_keys[1], (D,), jnp.float32), 0.5, 1.5)
    head = draw_head(jax.random.fold_in(arg_keys[5], 71), 0)
    targets = touch_ends(ranked_ids(arg_keys[3], (ROWS,), VOCAB, 2), jax.random.fold_in(arg_keys[3], 3), 0, VOCAB - 1).astype(jnp.int32)
    lengths = jax.vmap(lambda own: uneven(own, SEQ_DEV + 1, ROWS_DEV, MOST, 2))(jax.random.split(arg_keys[4], N_REQ)).reshape((N_REQ, SEQ_DEV + 1)).astype(jnp.int32)
    return {"hidden": hidden, "gain": gain, "head": head, "targets": targets, "lengths": lengths}


EPS = 1e-05

def reference(hidden, gain, head, targets, lengths):
    values = hidden.astype(jnp.float32)
    mean_sq = lax.optimization_barrier(jnp.sum(values * values, axis=1)) / D
    normed = (values * lax.rsqrt(mean_sq + EPS)[:, None] * gain[None, :]).astype(jnp.bfloat16)
    block = min(512, ROWS_DEV)
    count = ROWS // block

    def one_block(block_index):
        start = block_index * block
        rows_blk = lax.dynamic_slice_in_dim(normed, start, block, 0)
        logits = jnp.dot(rows_blk, head, preferred_element_type=jnp.float32)
        wanted = lax.dynamic_slice_in_dim(targets, start, block, 0)
        peak = lax.optimization_barrier(jnp.max(logits, axis=1))
        weights = jnp.exp(logits - peak[:, None])
        total = lax.optimization_barrier(jnp.sum(weights, axis=1))
        moment = lax.optimization_barrier(jnp.sum(weights * logits, axis=1))
        picked = jnp.take_along_axis(logits, wanted[:, None], axis=1)[:, 0]
        log_total = peak + jnp.log(total)
        return (picked - log_total, log_total - moment / total)
    logprob, entropy = lax.map(one_block, jnp.arange(count, dtype=jnp.int32))
    logprob = logprob.reshape(N_REQ, ROWS_DEV)
    entropy = entropy.reshape(N_REQ, ROWS_DEV)
    seq_lens = lengths[:, :SEQ_DEV].astype(jnp.int32)
    ends = jnp.cumsum(seq_lens, axis=1).astype(jnp.int32)
    starts = ends - seq_lens
    local = jnp.arange(ROWS_DEV, dtype=jnp.int32)
    valid = local[None, :] < ends[:, -1:]
    logprob = jnp.where(valid, logprob, 0.0)
    entropy = jnp.where(valid, entropy, 0.0)
    member = ((local[None, None, :] >= starts[:, :, None]) & (local[None, None, :] < ends[:, :, None])).astype(jnp.float32)
    divisor = seq_lens.astype(jnp.float32)
    seq_lp = lax.optimization_barrier(jnp.sum(member * logprob[:, None, :], axis=2)) / divisor
    seq_ent = lax.optimization_barrier(jnp.sum(member * entropy[:, None, :], axis=2)) / divisor
    return (logprob.reshape(ROWS), entropy.reshape(ROWS), seq_lp.reshape(SEQS), seq_ent.reshape(SEQS))
```

```python
import jax
import jax.numpy as jnp
from jax import lax
from jax.experimental import pallas as pl
from jax.experimental.pallas import tpu as pltpu
from jax.sharding import Mesh
from jax.sharding import PartitionSpec as P

SEQ_DEV = 3
VOCAB = ("vocab_0", "vocab_1", "vocab_2")
REQ_VOCAB = ("req", "vocab_0", "vocab_1", "vocab_2")
EPS = 1e-05

NZ, NX, NY = 8, 4, 4
F32, BF16, I32 = jnp.float32, jnp.bfloat16, jnp.int32
FIRST = 48

GROUPS = (0, 1, -1, 2, -2, 3, -3, 4)
HEAD_FROM = (0, 1, -1, 2)

ARRIVALS = (
    (0, 0, 1), (0, 0, -1), (0, 1, 0), (0, -1, 0), (1, 0, 1), (1, 0, -1), (1, 1, 0), (1, -1, 0),
    (0, 0, 2), (0, 1, 1), (0, -1, 1), (0, 1, -1), (0, -1, -1), (1, 0, 2), (1, 1, -1), (0, 2, 0),
    (0, -2, 0), (1, 1, 1), (1, -1, -1), (1, 2, 0), (1, -2, 0), (1, -1, 1), (0, 1, 2), (0, -1, 2),
    (1, 1, 2), (0, 2, 1), (0, -2, 1), (1, 2, -1), (0, 2, -1), (0, -2, -1), (1, 2, 1), (0, 3, 0),
    (0, -3, 0), (1, -2, -1), (1, -2, 1), (1, -1, 2), (1, 3, 0), (1, -3, 0), (1, 2, 2), (0, 2, 2),
    (0, -2, 2), (0, 3, 1), (0, -3, 1), (1, -2, 2), (1, 3, -1), (0, 3, -1), (0, -3, -1), (1, 3, 1),
    (0, 4, 0), (0, -3, 2), (1, -3, -1), (1, 4, 0), (1, -3, 1), (0, 3, 2), (1, 3, 2), (0, 4, 1),
    (0, 4, -1), (0, 4, 2), (1, 4, 1), (1, 4, -1), (1, -3, 2), (1, 4, 2),
)
HIDDEN_AT = {name: i for i, name in enumerate(ARRIVALS)}


HEADS = ((0, 1), (2, 3), (4, 5), (6,), (), (7,), (), ())


def schedule():
    steps, pending = [], list(ARRIVALS)
    for t, dz in enumerate(GROUPS):
        last = max([i for i, name in enumerate(pending) if name[1] == dz], default=-1)
        here, pending = pending[: last + 1], pending[last + 1 :]
        heads = [("y", (s, dy)) for s in HEADS[t] for dy in (1, -1, 2)]
        placed = [(k / max(1, len(here)), ("h", name)) for k, name in enumerate(here)]
        placed += [((k + 1) / (len(heads) + 1), head) for k, head in enumerate(heads)]
        placed.sort(key=lambda item: item[0])
        steps.append([event for _, event in placed] + [("p", (t, dy)) for dy in HEAD_FROM])
    assert not pending
    return steps


def kernel(
    hid, gain, head, targets, lengths, out,
    H, W, acc, staged, squares, st_out, st_in, sx_out, sx_in, fin, fin_other,
    local_sem, hid_send, hid_recv, own_send, own_recv, y_send, y_recv, p_send, p_recv,
    z_send, z_recv, x_send, x_recv, f_send, f_recv, c_send, c_recv,
):
    y, z = lax.axis_index("req"), lax.axis_index("vocab_0")
    x, c = lax.axis_index("vocab_1"), lax.axis_index("vocab_2")
    way = 1 - 2 * c

    def at(y_to, z_to, x_to, c_to):
        return {"req": y_to, "vocab_0": z_to, "vocab_1": x_to, "vocab_2": c_to}

    def zof(d):
        return (z + NZ + way * d) % NZ

    def xof(d):
        return (x + NX + way * d) % NX

    def yof(d):
        return (y + NY + way * d) % NY

    partner = at(y, z, x, 1 - c)

    def remote(src, dst, send_sem, recv_sem, to):
        return pltpu.make_async_remote_copy(
            src_ref=src, dst_ref=dst, send_sem=send_sem, recv_sem=recv_sem,
            device_id=to, device_id_type=pl.DeviceIdType.MESH,
        )

    mine = pl.multiple_of(c * 1024, 1024)
    other = pl.multiple_of((1 - c) * 1024, 1024)
    own_rows = pl.ds(pl.multiple_of(c * 64, 64), 64)
    load_hid = pltpu.make_async_copy(
        hid.at[:, pl.ds(mine, 1024)], H.at[z, x, own_rows, :], local_sem.at[0]
    )
    load_head = pltpu.make_async_copy(head, staged, local_sem.at[1])
    load_hid.start()
    load_head.start()

    barrier = pltpu.get_barrier_semaphore()
    peers = [at(y, (z + k) % NZ, x, c) for k in range(1, NZ)]
    peers += [at(y, z, (x + k) % NX, c) for k in range(1, NX)]
    peers += [partner, at(yof(1), z, x, c), at(yof(-1), z, x, c)]
    for peer in peers:
        pl.semaphore_signal(barrier, inc=1, device_id=peer, device_id_type=pl.DeviceIdType.MESH)
    pl.semaphore_wait(barrier, len(peers))

    own_copy = remote(
        hid.at[:, pl.ds(other, 1024)], H.at[z, x, own_rows, :],
        own_send.at[0], own_recv.at[0], partner,
    )
    own_copy.start()
    load_hid.wait()
    own_copy.wait_recv()

    def piece(name):
        kind, dz, dx = name
        rows = pl.ds(0, FIRST) if kind == 0 else pl.ds(FIRST, 128 - FIRST)
        return H.at[zof(-dz), xof(-dx), rows, :]

    def hidden_copy(name, hop):
        kind, dz, dx = name
        ez, ex = hop
        k = HIDDEN_AT[(kind, dz + ez, dx + ex)]
        to = at(y, zof(ez), xof(ex), c)
        return remote(piece(name), piece(name), hid_send.at[k], hid_recv.at[k], to)

    def hops(name):
        kind, dz, dx = name
        along_x = [(0, 1), (0, -1)] if dx == 0 else [(0, 1)] if dx == 1 else []
        along_z = [(1, 0), (-1, 0)] if dz == 0 else [(1, 0)] if 0 < dz < 4 else []
        along_z = [(-1, 0)] if dz in (-1, -2) else along_z
        if kind == 0:
            return (along_x if dz == 0 else []) + along_z
        return (along_z if dx == 0 else []) + along_x

    def forward(name):
        for hop in hops(name):
            hidden_copy(name, hop).start()

    def take_hidden(name):
        k = HIDDEN_AT[name]
        remote(piece(name), piece(name), hid_send.at[k], hid_recv.at[k], partner).wait_recv()
        forward(name)

    forward((1, 0, 0))
    forward((0, 0, 0))

    load_head.wait()
    own_cols = y * 2 + c

    def stage(s, carry):
        cols = pl.ds(pl.multiple_of(s * 512, 512), 512)
        block = staged[cols, :].astype(F32).T
        W[own_cols, s] = (block * (gain[:, cols] * (2.0 ** -9))).astype(BF16)
        return carry

    lax.fori_loop(0, 8, stage, 0)

    def slab(t, dy, core):
        return W.at[yof(-dy) * 2 + core, zof(-GROUPS[t])]

    def y_index(t, dy):
        return t * 3 + (0, 1, 2)[(1, -1, 2).index(dy)]

    def send_y(t, dy, hop):
        k = y_index(t, dy + hop)
        to = at(yof(hop), z, x, c)
        return remote(slab(t, dy, c), slab(t, dy, c), y_send.at[k], y_recv.at[k], to)

    def send_p(t, dy):
        mirror = GROUPS.index(-GROUPS[t]) if abs(GROUPS[t]) < 4 else t
        k = mirror * 4 + HEAD_FROM.index(-dy if dy < 2 else dy)
        return remote(slab(t, dy, c), slab(t, dy, c), p_send.at[k], p_recv.at[k], partner)

    def own_slab(t):
        send_y(t, 0, 1).start()
        send_y(t, 0, -1).start()
        send_p(t, 0).start()

    def take_y(t, dy):
        k = y_index(t, dy)
        ref = slab(t, dy, c)
        remote(ref, ref, y_send.at[k], y_recv.at[k], partner).wait_recv()
        if dy == 1:
            send_y(t, 1, 1).start()
            if t + 2 < 8:
                own_slab(t + 2)
        send_p(t, dy).start()

    def take_p(t, dy):
        k = t * 4 + HEAD_FROM.index(dy)
        ref = slab(t, dy, 1 - c)
        remote(ref, ref, p_send.at[k], p_recv.at[k], partner).wait_recv()

    own_slab(0)
    own_slab(1)

    acc[...] = jnp.zeros((1024, 1024), F32)
    squares[...] = jnp.zeros((8, 1024), F32)
    steps = schedule()

    def step(t, carry):
        for k, events in enumerate(steps):

            @pl.when(t == k)
            def _():
                for kind, what in events:
                    {"h": take_hidden, "y": lambda w: take_y(*w), "p": lambda w: take_p(*w)}[kind](what)

        sign = 1 - 2 * (t % 2)
        group = (z + 2 * NZ + way * sign * ((t + 1) // 2)) % NZ

        acc[...] += jnp.dot(
            W[:, group].reshape(1024, 512), H[group].reshape(512, 1024),
            preferred_element_type=F32,
        )

        def square(i, total):
            v = H[group, i // 4, pl.ds(pl.multiple_of((i % 4) * 32, 32), 32), :].astype(F32)
            return total + jnp.sum((v * v).reshape(4, 8, 1024), axis=0)

        squares[...] = lax.fori_loop(0, 16, square, squares[...])
        return carry

    lax.fori_loop(0, 8, step, 0)

    mean_sq = jnp.sum(squares[...], axis=0, keepdims=True) / 4096.0
    scale = lax.rsqrt(mean_sq + EPS) * 512.0

    def highest(i, best):
        v = acc[pl.ds(pl.multiple_of(i * 32, 32), 32), :]
        return jnp.maximum(best, jnp.max(v.reshape(4, 8, 1024), axis=0))

    top = lax.fori_loop(1, 32, highest, jnp.max(acc[0:32, :].reshape(4, 8, 1024), axis=0))
    peak = jnp.max(top, axis=0, keepdims=True) * scale
    wanted = targets[:, pl.ds(mine, 1024)]
    in_y = wanted // 8192
    in_p = (wanted // 256) % 32
    local = jnp.where(in_p == z * 4 + x, in_y * 256 + wanted % 256, -1)
    for part in range(4):
        lanes = slice(part * 256, part * 256 + 256)
        scale_b = jnp.broadcast_to(scale[:, lanes], (8, 256))
        peak_b = jnp.broadcast_to(peak[:, lanes], (8, 256))
        local_b = jnp.broadcast_to(local[:, lanes], (8, 256)) - lax.broadcasted_iota(I32, (8, 256), 0)

        def sums(i, carry):
            total, moment, picked = carry
            for j in range(4):
                row = pl.multiple_of(i * 32 + j * 8, 8)
                logit = acc[pl.ds(row, 8), lanes] * scale_b
                weight = jnp.exp(logit - peak_b)
                total = total + weight
                moment = moment + weight * logit
                picked = picked + jnp.where(local_b == row, logit, 0.0)
            return total, moment, picked

        zero = jnp.zeros((8, 256), F32)
        total, moment, picked = lax.fori_loop(0, 32, sums, (zero, zero, zero))
        for k in range(2):
            cut = slice(k * 128, k * 128 + 128)
            for row, value in enumerate((total, moment, picked)):
                st_out[part * 2 + k, row + 1 : row + 2, :] = jnp.sum(value[:, cut], axis=0, keepdims=True)
            st_out[part * 2 + k, 0:1, :] = peak[:, part * 256 + k * 128 : part * 256 + k * 128 + 128]

    def combine(tiles):
        tops = tiles[:, 0, :]
        most = jnp.max(tops, axis=0, keepdims=True)
        factor = jnp.exp(tops - most)
        return (
            most,
            jnp.sum(tiles[:, 1, :] * factor, axis=0, keepdims=True),
            jnp.sum(tiles[:, 2, :] * factor, axis=0, keepdims=True),
            jnp.sum(tiles[:, 3, :], axis=0, keepdims=True),
        )

    def z_copy(k):
        return remote(
            st_out.at[(z + k) % NZ], st_in.at[z], z_send.at[k], z_recv.at[k], at(y, (z + k) % NZ, x, c)
        )

    for k in range(1, NZ):
        z_copy(k).start()
    st_in[z] = st_out[z]
    for k in range(1, NZ):
        ref = st_in.at[(z + NZ - k) % NZ]
        remote(ref, ref, z_send.at[k], z_recv.at[k], partner).wait_recv()
    for row, value in enumerate(combine(st_in)):
        sx_out[row : row + 1, :] = value

    def x_copy(k):
        return remote(
            sx_out, sx_in.at[x], x_send.at[k], x_recv.at[k], at(y, z, (x + k) % NX, c)
        )

    for k in range(1, NX):
        x_copy(k).start()
    sx_in[x] = sx_out[...]
    for k in range(1, NX):
        ref = sx_in.at[(x + NX - k) % NX]
        remote(ref, ref, x_send.at[k], x_recv.at[k], partner).wait_recv()
    top_all, total_all, moment_all, picked_all = combine(sx_in)
    log_total = top_all + jnp.log(total_all)
    lens = [lengths[0, k] for k in range(SEQ_DEV)]
    ends = [lens[0], lens[0] + lens[1], lens[0] + lens[1] + lens[2]]
    row_ids = c * 1024 + z * 128 + lax.broadcasted_iota(I32, (1, 128), 1)
    valid = row_ids < ends[2]
    fin[z, 0:1, :] = jnp.where(valid, picked_all - log_total, 0.0)
    fin[z, 1:2, :] = jnp.where(valid, log_total - moment_all / total_all, 0.0)

    def f_copy(k):
        return remote(fin.at[z], fin.at[z], f_send.at[k], f_recv.at[k], at(y, (z + k) % NZ, x, c))

    for k in range(1, NZ):
        f_copy(k).start()
    for k in range(1, NZ):
        ref = fin.at[(z + NZ - k) % NZ]
        remote(ref, ref, f_send.at[k], f_recv.at[k], partner).wait_recv()
    c_copy = remote(fin, fin_other, c_send.at[0], c_recv.at[0], partner)
    c_copy.start()
    c_copy.wait_recv()

    lane = lax.broadcasted_iota(I32, (1, 128), 1)
    tile = ((z % 4) * 4 + x) // 2
    shift = (128 - (64 * (x % 2) + 32 * c)) % 128
    here = jnp.where(z // 4 == c, fin[tile], fin_other[tile])
    out[...] = pltpu.roll(here, shift, 1)
    ids = lax.broadcasted_iota(I32, (8, 128), 0) * 128 + lax.broadcasted_iota(I32, (8, 128), 1)
    for row in range(2):
        line = jnp.zeros((1, 128), F32)
        for k in range(SEQ_DEV):
            start = ends[k] - lens[k]
            parts = []
            for values, first in ((fin[:, row, :], mine), (fin_other[:, row, :], other)):
                rows = ids + first
                inside = (rows >= start) & (rows < ends[k])
                kept = jnp.where(inside, values, 0.0)
                parts.append(jnp.sum(jnp.sum(kept, axis=0, keepdims=True), axis=1, keepdims=True))
            mean = (parts[0] + parts[1]) / jnp.broadcast_to(lens[k].astype(F32), (1, 1))
            line = jnp.where(lane == k, mean, line)
        out[2 + row : 3 + row, :] = line

    own_copy.wait_send()
    for name in [(0, 0, 0), (1, 0, 0), *ARRIVALS]:
        for hop in hops(name):
            hidden_copy(name, hop).wait_send()
    for t in range(8):
        send_y(t, 0, 1).wait_send()
        send_y(t, 0, -1).wait_send()
        send_y(t, 1, 1).wait_send()
        for dy in HEAD_FROM:
            send_p(t, dy).wait_send()
    for k in range(1, NZ):
        z_copy(k).wait_send()
        f_copy(k).wait_send()
    for k in range(1, NX):
        x_copy(k).wait_send()
    c_copy.wait_send()


def shards(hidden, gain, head, targets, lengths):
    dma = pltpu.SemaphoreType.DMA
    n = len(ARRIVALS)
    vmem = pl.BlockSpec(memory_space=pltpu.VMEM)
    tile = pl.pallas_call(
        kernel,
        out_shape=jax.ShapeDtypeStruct((8, 128), F32),
        in_specs=[
            pl.BlockSpec(memory_space=pl.ANY), vmem, pl.BlockSpec(memory_space=pl.ANY), vmem,
            pl.BlockSpec(memory_space=pltpu.SMEM),
        ],
        out_specs=vmem,
        scratch_shapes=[
            pltpu.VMEM((NZ, NX, 128, 1024), BF16),
            pltpu.VMEM((8, 8, 128, 512), BF16),
            pltpu.VMEM((1024, 1024), F32),
            pltpu.VMEM((4096, 128), BF16),
            pltpu.VMEM((8, 1024), F32),
            pltpu.VMEM((NZ, 8, 128), F32),
            pltpu.VMEM((NZ, 8, 128), F32),
            pltpu.VMEM((8, 128), F32),
            pltpu.VMEM((NX, 8, 128), F32),
            pltpu.VMEM((NZ, 8, 128), F32),
            pltpu.VMEM((NZ, 8, 128), F32),
            dma((2,)), dma((n,)), dma((n,)), dma((1,)), dma((1,)), dma((24,)), dma((24,)),
            dma((32,)), dma((32,)), dma((8,)), dma((8,)), dma((4,)), dma((4,)), dma((8,)), dma((8,)),
            dma((1,)), dma((1,)),
        ],
        compiler_params=pltpu.CompilerParams(
            collective_id=0, has_side_effects=True, vmem_limit_bytes=48 * 1024 * 1024
        ),
        name="rollout_stats",
    )(hidden.T, gain.reshape(1, 4096), head, targets.reshape(1, 2048), lengths)
    return tile[0, :32], tile[1, :32], tile[2, :SEQ_DEV], tile[3, :SEQ_DEV]


def solution(mesh):
    split = Mesh(
        mesh.devices.reshape(mesh.shape["req"], NZ, NX, 2), ("req", "vocab_0", "vocab_1", "vocab_2")
    )
    placed = (P("req", VOCAB), P(), P(None, REQ_VOCAB), P("req"), P("req", None))
    return jax.shard_map(
        shards,
        mesh=split,
        in_specs=placed,
        out_specs=(P(REQ_VOCAB), P(REQ_VOCAB), P("req"), P("req")),
        check_vma=False,
    )
```
